256 devices in a mesh: ctx: 128 (over y, x, z), tp: 2 (over core).
Axes of the slice: x: 4, y: 4, z: 8, core: 2. Of those that a mesh axis runs over, the one named last changes fastest.
Arguments:
- hidden: bfloat16 [32768, 4096], P('ctx', 'tp'), may hold values from -6 to 6
- w_query: bfloat16 [4096, 4096], P('ctx', 'tp'), may hold values from -0.09375 to 0.09375
- key_weight: bfloat16 [4096, 256], P('ctx', 'tp'), may hold values from -0.09375 to 0.09375
- value_weight: bfloat16 [4096, 256], P('ctx', 'tp'), may hold values from -0.09375 to 0.09375
- q_gain: float32 [128], replicated, may hold values from 0.5 to 2
- key_norm_gain: float32 [128], replicated, may hold values from 0.5 to 2
- earlier_keys: bfloat16 [131072, 256], P('ctx', 'tp'), may hold values from -288 to 288
- earlier_values: bfloat16 [131072, 256], P('ctx', 'tp'), may hold values from -6 to 6
- counts: int32 [64], replicated, may hold values from 1 to 16, as said below
- place: int32 [64, 16], replicated, may hold values from 0 to 15, as said below
Outputs:
- attended: bfloat16 [32768, 4096], P('ctx', 'tp')
- new_keys: bfloat16 [32768, 256], P('ctx', 'tp')
- new_values: bfloat16 [32768, 256], P('ctx', 'tp')
The draws below stay inside these ranges and needn't reach their ends.
Inputs may be any that keep to these rules, and one draw needn't show every extreme that they name: `counts`: 16 for one trajectory and 1 for another in every draw; most trajectories have few blocks. `place`: each row orders all 16 slots of the trajectory; the slots after the first counts[b] hold stale data.
All inputs are finite; a program needn't handle non-finite values.
Results may differ from the reference program's by a relative error of at most 0.007.
Values may be sent and summed in bfloat16 or wider, within the bound.
A program may use at most 64 MiB of HBM per device.

```python
import math
import jax
import jax.numpy as jnp
from jax import lax

MODEL_WIDTH = 4096
QUERY_HEADS = 32
KEY_VALUE_HEADS = 2
HEAD_SIZE = 128
BLOCK_TOKENS = 128
BLOCK_SLOTS = 8
NEW_PER_PATH = 512
TRAJ = 64
NEW_TOKEN_TOTAL = 32768
MAXB = 16
N_CTX = 128


def draw_earlier_keys(key, part):
    leading_index = jax.random.fold_in(key, 0)
    start_offset = jnp.clip(jax.random.normal(leading_index, (N_CTX * BLOCK_SLOTS * BLOCK_TOKENS, KEY_VALUE_HEADS * HEAD_SIZE), jnp.float32), -6.0, 6.0)
    return start_offset.astype(jnp.bfloat16)


def draw_counts(key, part):
    leading_index, second, third = jax.random.split(jax.random.fold_in(key, 11), 3)
    early = jax.random.randint(leading_index, (TRAJ,), 1, MAXB + 1)
    later = jax.random.randint(second, (TRAJ,), 1, MAXB + 1)
    blocks = jnp.minimum(early, later)
    order = jax.random.permutation(third, TRAJ)
    blocks = blocks.at[order[0]].set(MAXB)
    blocks = blocks.at[order[1]].set(1)
    return blocks.astype(jnp.int32)


def draw_place(key, part):
    streams = jax.random.split(jax.random.fold_in(key, 23), TRAJ)
    return jax.vmap(lambda stream: jax.random.permutation(stream, MAXB))(streams).astype(jnp.int32)


def shard_levels(own_key, shape, cuts, low, high):
    loudness, own = 1.0, jax.random.fold_in(own_key, 6)
    for dim, shards_of in cuts:
        steps = jnp.exp(jax.random.uniform(jax.random.fold_in(own, dim), (shards_of,), jnp.float32, low / len(cuts), high / len(cuts)))
        loudness = loudness * jnp.repeat(steps, shape[dim] // shards_of).reshape([-1 if axis == dim else 1 for axis in range(len(shape))])
    return loudness


def scatter_about(stream_key, extent, scale, limit, shards=(), kind=jnp.bfloat16):
    entries = jax.random.normal(stream_key, extent, jnp.float32) * scale
    if len(shards) > 0:
        entries = shard_levels(stream_key, extent, shards, -0.22, 0.18) * entries
    return jnp.clip(entries, min=-limit, max=limit).astype(kind)


def setup_inputs(seed: int = 0) -> dict:
    splits = jax.random.split(jax.random.key(seed), 11)
    hidden = scatter_about(splits[0], (NEW_TOKEN_TOTAL, MODEL_WIDTH), 1.0, 6.0, ((0, 128), (1, 2)))
    w_query = scatter_about(splits[1], (MODEL_WIDTH, QUERY_HEADS * HEAD_SIZE), MODEL_WIDTH ** -0.5, 0.09375, ((0, 128), (1, 2)))
    key_weight = scatter_about(splits[2], (MODEL_WIDTH, KEY_VALUE_HEADS * HEAD_SIZE), MODEL_WIDTH ** -0.5, 0.09375, ((0, 128), (1, 2)))
    value_weight = scatter_about(splits[3], (MODEL_WIDTH, KEY_VALUE_HEADS * HEAD_SIZE), MODEL_WIDTH ** -0.5, 0.09375, ((0, 128), (1, 2)))
    q_gain = jnp.clip(jnp.exp(jax.random.uniform(splits[4], (HEAD_SIZE,), jnp.float32, math.log(0.5), math.log(2.0))), 0.5, 2.0)
    key_norm_gain = jnp.clip(jnp.exp(jax.random.uniform(splits[5], (HEAD_SIZE,), jnp.float32, math.log(0.5), math.log(2.0))), 0.5, 2.0)
    earlier_keys = draw_earlier_keys(jax.random.fold_in(splits[10], 71), 0)
    earlier_values = scatter_about(splits[7], (N_CTX * BLOCK_SLOTS * BLOCK_TOKENS, KEY_VALUE_HEADS * HEAD_SIZE), 1.0, 6.0, ((0, 128), (1, 2)))
    counts = draw_counts(jax.random.fold_in(splits[10], 71), 0)
    place = draw_place(jax.random.fold_in(splits[10], 71), 0)
    return {"hidden": hidden, "w_query": w_query, "key_weight": key_weight, "value_weight": value_weight, "q_gain": q_gain, "key_norm_gain": key_norm_gain, "earlier_keys": earlier_keys, "earlier_values": earlier_values, "counts": counts, "place": place}


def normalize_and_turn(values, gain, token_position):
    width = values.shape[-1]
    half = width // 2
    scaled = values * lax.rsqrt(lax.optimization_barrier(jnp.mean(values * values, axis=-1, keepdims=True)) + 1e-06) * gain
    freq = jnp.exp(jnp.arange(half, dtype=jnp.float32) * (-2.0 / width) * math.log(1000000.0))
    angle = token_position.astype(jnp.float32)[:, None] * freq[None, :]
    cosine = jnp.cos(angle)[:, None, :]
    sine = jnp.sin(angle)[:, None, :]
    leading_index = scaled[..., :half]
    second = scaled[..., half:]
    return jnp.concatenate([leading_index * cosine - second * sine, second * cosine + leading_index * sine], axis=-1)

def reference(hidden, w_query, key_weight, value_weight, q_gain, key_norm_gain, earlier_keys, earlier_values, counts, place):
    query = jnp.dot(hidden, w_query, preferred_element_type=jnp.float32)
    key_projected = jnp.dot(hidden, key_weight, preferred_element_type=jnp.float32)
    value_projected = jnp.dot(hidden, value_weight, preferred_element_type=jnp.float32)
    row_ids = jnp.arange(NEW_TOKEN_TOTAL, dtype=jnp.int32)
    token_position = counts[row_ids // NEW_PER_PATH] * BLOCK_TOKENS + row_ids % NEW_PER_PATH
    rotated = normalize_and_turn(query.reshape(NEW_TOKEN_TOTAL, QUERY_HEADS, HEAD_SIZE), q_gain, token_position).astype(jnp.bfloat16)
    fresh_keys = normalize_and_turn(key_projected.reshape(NEW_TOKEN_TOTAL, KEY_VALUE_HEADS, HEAD_SIZE), key_norm_gain, token_position).astype(jnp.bfloat16)
    fresh_values = value_projected.astype(jnp.bfloat16).reshape(NEW_TOKEN_TOTAL, KEY_VALUE_HEADS, HEAD_SIZE)
    query_group = QUERY_HEADS // KEY_VALUE_HEADS
    token_extent = MAXB * BLOCK_TOKENS

    def one_traj(index):
        start = (index * NEW_PER_PATH).astype(jnp.int32)
        query_slice = lax.dynamic_slice_in_dim(rotated, start, NEW_PER_PATH, 0).astype(jnp.float32)
        key_part = lax.dynamic_slice_in_dim(fresh_keys, start, NEW_PER_PATH, 0)
        value_part = lax.dynamic_slice_in_dim(fresh_values, start, NEW_PER_PATH, 0)
        start_offset = (index * token_extent).astype(jnp.int32)
        gathered_keys = lax.dynamic_slice_in_dim(earlier_keys, start_offset, token_extent, 0).reshape(token_extent, KEY_VALUE_HEADS, HEAD_SIZE)
        gathered_values = lax.dynamic_slice_in_dim(earlier_values, start_offset, token_extent, 0).reshape(token_extent, KEY_VALUE_HEADS, HEAD_SIZE)
        order = place[index]
        used = jnp.arange(MAXB, dtype=jnp.int32) < counts[index]
        live = jnp.any((order[:, None] == jnp.arange(MAXB, dtype=jnp.int32)[None, :]) & used[:, None], axis=0)
        live_tok = jnp.repeat(live, BLOCK_TOKENS)
        keys_all = jnp.concatenate([gathered_keys, key_part], axis=0).astype(jnp.float32)
        vals_all = jnp.concatenate([gathered_values, value_part], axis=0).astype(jnp.float32)
        offsets = jnp.arange(NEW_PER_PATH, dtype=jnp.int32)
        causal = offsets[None, :] <= offsets[:, None]
        allowed = jnp.concatenate([jnp.broadcast_to(live_tok[None, :], (NEW_PER_PATH, token_extent)), causal], axis=1)
        group_queries = query_slice.reshape(NEW_PER_PATH, KEY_VALUE_HEADS, query_group, HEAD_SIZE)
        score = jnp.einsum('ckgd,nkd->kgcn', group_queries, keys_all) * HEAD_SIZE ** (-0.5)
        score = jnp.where(allowed[None, None], score, -jnp.inf)
        top = lax.optimization_barrier(jnp.max(score, axis=-1, keepdims=True))
        weight = jnp.exp(score - top)
        total = lax.optimization_barrier(jnp.sum(weight, axis=-1, keepdims=True))
        rounded = weight.astype(jnp.bfloat16).astype(jnp.float32)
        mixed = jnp.einsum('kgcn,nkd->kgcd', rounded, vals_all) / total
        return jnp.transpose(mixed, (2, 0, 1, 3)).reshape(NEW_PER_PATH, QUERY_HEADS * HEAD_SIZE).astype(jnp.bfloat16)
    attended = lax.map(one_traj, jnp.arange(TRAJ, dtype=jnp.int32)).reshape(NEW_TOKEN_TOTAL, QUERY_HEADS * HEAD_SIZE)
    return (attended, fresh_keys.reshape(NEW_TOKEN_TOTAL, KEY_VALUE_HEADS * HEAD_SIZE), fresh_values.reshape(NEW_TOKEN_TOTAL, KEY_VALUE_HEADS * HEAD_SIZE))
```

```python
import functools
import math

import jax
import jax.numpy as jnp
from jax import lax
from jax.experimental import pallas as pl
from jax.experimental.pallas import tpu as pltpu
from jax.sharding import PartitionSpec as P

MESH = pl.DeviceIdType.MESH
HEAD = 128
BLOCK = 128
TOK = 256
NY, NX, NZ = 4, 4, 8
SLOTS = 16
CACHE = SLOTS * BLOCK
KEYS = CACHE + 2 * TOK
FACTOR = HEAD**-0.5 * math.log2(math.e)
NEG = -1e30


def kernel(
    counts, place, hid, wq, kw, vw, qg, kg, ck, cv,
    att, nk, nv,
    H, W, KC, VC, KN, VN, KM, VM, QS, QA, COS, SIN, TRI, O,
    local_sem, out_sem,
    p0_s, p0_r, h_s, h_r, c_s, c_r, kv_s, kv_r, za_s, za_r, xa_s, xa_r, xb_s, xb_r, zb_s, zb_r, q_s, q_r,
):
    i = lax.axis_index("ctx")
    c = lax.axis_index("tp")
    y, x, z = i // (NX * NZ), (i // NZ) % NX, i % NZ
    zp = z % 2
    sent = []

    def ym(k):
        return (y + k + NY) % NY

    def xm(k):
        return (x + k + NX) % NX

    def zm(k):
        return (z + k + NZ) % NZ

    def at(dy=0, dx=0, dz=0):
        return (ym(dy) * (NX * NZ) + xm(dx) * NZ + zm(dz), c)

    other_core = (i, 1 - c)
    pair = (i + 1 - 2 * zp, c)

    def send(src, dst, s, r, device):
        copy = pltpu.make_async_remote_copy(
            src_ref=src, dst_ref=dst, send_sem=s, recv_sem=r, device_id=device, device_id_type=MESH
        )
        copy.start()
        sent.append(copy)

    def arrived(dst, s, r):
        pltpu.make_async_remote_copy(
            src_ref=dst, dst_ref=dst, send_sem=s, recv_sem=r, device_id=other_core, device_id_type=MESH
        ).wait_recv()

    local = []

    def bring(src, dst):
        copy = pltpu.make_async_copy(src, dst, local_sem.at[len(local)])
        copy.start()
        local.append(copy)

    def columns(yb, g):
        return pl.ds(pl.multiple_of(yb * 512 + (g - 1) * 256, 256), 256)

    bring(wq.at[:, columns(y, 1)], W.at[1, y, x, z])
    bring(kw, W.at[0, y, x, z, :, pl.ds(0, 128)])
    bring(vw, W.at[0, y, x, z, :, pl.ds(128, 128)])
    bring(wq.at[:, columns(y, 2)], W.at[2, y, x, z])
    bring(hid, H.at[y, c])
    bring(ck, KC.at[zp])
    bring(cv, VC.at[zp])

    barrier = pltpu.get_barrier_semaphore()
    for device in (at(dy=1), at(dy=-1), at(dy=2), at(dx=1), at(dx=-1), at(dz=1), at(dz=-1), other_core):
        pl.semaphore_signal(barrier, inc=1, device_id=device, device_id_type=MESH)
    pl.semaphore_wait(barrier, 8)

    steps_y = (1, -1, 2)
    for g in (1, 0, 2):
        for n, dy in enumerate(steps_y):
            if g == 0:
                for m, part in enumerate((kw, vw)):
                    send(part, W.at[0, y, x, z, :, pl.ds(128 * m, 128)], p0_s.at[n, 2 + m], p0_r.at[n, 2 + m], at(dy=dy))
            else:
                send(wq.at[:, columns(ym(dy), g)], W.at[g, y, x, z], p0_s.at[n, g - 1], p0_r.at[n, g - 1], at(dy=dy))

    def own_rows(g):
        for n, dy in enumerate(steps_y):
            if g == 0:
                for m in range(2):
                    arrived(W.at[0, ym(-dy), x, z, :, pl.ds(128 * m, 128)], p0_s.at[n, 2 + m], p0_r.at[n, 2 + m])
            else:
                arrived(W.at[g, ym(-dy), x, z], p0_s.at[n, g - 1], p0_r.at[n, g - 1])

    def half(n):
        return pl.ds(128 * n, 128)

    for n in (0, 1):
        send(hid.at[half(n)], H.at[y, c, half(n)], h_s.at[0, n], h_r.at[0, n], at(dy=1))
        send(hid.at[half(1 - n)], H.at[y, c, half(1 - n)], h_s.at[1, 1 - n], h_r.at[1, 1 - n], at(dy=-1))
    send(hid, H.at[y, c], c_s.at[0], c_r.at[0], other_core)

    def h_arrived(d, n):
        arrived(H.at[ym(-1 if d == 0 else 1), c, half(n)], h_s.at[d, n], h_r.at[d, n])

    def h_forward(d):
        yb = ym(-1 if d == 0 else 1)
        send(H.at[yb, c, half(d)], H.at[yb, c, half(d)], h_s.at[2, d], h_r.at[2, d], at(dy=1 if d == 0 else -1))

    def h_far_arrived(d):
        arrived(H.at[ym(2), c, half(d)], h_s.at[2, d], h_r.at[2, d])

    def h_to_core(yb, slot, rows=None):
        ref = H.at[yb, c] if rows is None else H.at[yb, c, rows]
        send(ref, ref, c_s.at[slot], c_r.at[slot], other_core)

    def h_from_core(yb, slot, rows=None):
        ref = H.at[yb, 1 - c] if rows is None else H.at[yb, 1 - c, rows]
        arrived(ref, c_s.at[slot], c_r.at[slot])

    def order(j):
        return zm((0, -1, 1, -2, 2, -3, 3, 4)[j])

    def a_block(g, xx, zz, hop=1, d=0):
        if hop == 4:
            return W.at[g, pl.ds(2 * d, 2), xx, zz]
        return W.at[g, :, xx, zz]

    def a_zsend(g, d, hop):
        sign = 1 - 2 * d
        ref = a_block(g, x, zm(-sign * (hop - 1)), hop, d)
        send(ref, ref, za_s.at[g - 1, d, hop - 1], za_r.at[g - 1, d, hop - 1], at(dz=sign))

    def a_zwait(g, d, hop):
        sign = 1 - 2 * d
        arrived(a_block(g, x, zm(-sign * hop), hop, d), za_s.at[g - 1, d, hop - 1], za_r.at[g - 1, d, hop - 1])

    def a_xsend(g, j):
        for d in (0, 1):
            ref = a_block(g, x, order(j))
            send(ref, ref, xa_s.at[g - 1, d, j], xa_r.at[g - 1, d, j], at(dx=1 - 2 * d))

    def a_xwait(g, d, j):
        arrived(a_block(g, xm(2 * d - 1), order(j)), xa_s.at[g - 1, d, j], xa_r.at[g - 1, d, j])

    def a_xforward(g, j):
        d = j % 2
        a_xwait(g, d, j)
        ref = a_block(g, xm(2 * d - 1), order(j))
        send(ref, ref, xa_s.at[g - 1, 2, j], xa_r.at[g - 1, 2, j], at(dx=1 - 2 * d))

    def a_step(g, n):
        if n == 0:
            own_rows(g)
            a_zsend(g, 0, 1)
            a_zsend(g, 1, 1)
            a_xsend(g, 0)
        elif n <= 3:
            for d in (0, 1):
                a_zwait(g, d, n)
                a_zsend(g, d, n + 1)
            for d in (0, 1):
                a_xsend(g, 2 * n - 1 + d)
            for j in ((0,), (1, 2), (3, 4))[n - 1]:
                a_xforward(g, j)
        elif n == 4:
            a_zwait(g, 0, 4)
            a_zwait(g, 1, 4)
            a_xsend(g, 7)
            a_xforward(g, 5)
            a_xforward(g, 6)
        elif n == 5:
            a_xforward(g, 7)
        else:
            for j in range(8):
                a_xwait(g, 1 - j % 2, j)
                arrived(a_block(g, xm(2), order(j)), xa_s.at[g - 1, 2, j], xa_r.at[g - 1, 2, j])

    far = (0, -1, 1, 2)

    def b_zsend(n, hop):
        for d in (0, 1):
            sign = 1 - 2 * d
            ref = a_block(0, xm(far[n]), zm(-sign * (hop - 1)), hop, d)
            send(ref, ref, zb_s.at[n, d, hop - 1], zb_r.at[n, d, hop - 1], at(dz=sign))

    def b_zwait(n, hop):
        for d in (0, 1):
            sign = 1 - 2 * d
            arrived(a_block(0, xm(far[n]), zm(-sign * hop), hop, d), zb_s.at[n, d, hop - 1], zb_r.at[n, d, hop - 1])

    def b_step(n):
        if n == 0:
            own_rows(0)
            for d in (0, 1):
                ref = a_block(0, x, z)
                send(ref, ref, xb_s.at[d], xb_r.at[d], at(dx=1 - 2 * d))
            b_zsend(0, 1)
        elif n == 1:
            for d in (0, 1):
                arrived(a_block(0, xm(2 * d - 1), z), xb_s.at[d], xb_r.at[d])
                ref = a_block(0, xm(2 * d - 1), z, 4, d)
                send(ref, ref, xb_s.at[2 + d], xb_r.at[2 + d], at(dx=1 - 2 * d))
            b_zsend(1, 1)
            b_zsend(2, 1)
        elif n == 2:
            for d in (0, 1):
                arrived(a_block(0, xm(2), z, 4, d), xb_s.at[2 + d], xb_r.at[2 + d])
            b_zsend(3, 1)
        elif n <= 5:
            for m in range(4):
                b_zwait(m, n - 2)
                b_zsend(m, n - 1)
        else:
            for m in range(4):
                b_zwait(m, 4)

    def trajectory(yb):
        return (yb * (NX * NZ) + x * NZ + z) // 2

    lane = lax.broadcasted_iota(jnp.int32, (TOK, HEAD), 1)
    freq = jnp.exp((lane % 64).astype(jnp.float32) * (-2.0 / HEAD) * math.log(1000000.0))

    def tables(yb):
        start = counts[trajectory(yb)] * BLOCK + zp * TOK
        pos = (start + lax.broadcasted_iota(jnp.int32, (TOK, HEAD), 0)).astype(jnp.float32)
        angle = pos * freq
        COS[yb] = jnp.cos(angle)
        SIN[yb] = jnp.where(lane < 64, -1.0, 1.0) * jnp.sin(angle)

    def turned(v, gain, yb):
        v = v * lax.rsqrt(jnp.mean(v * v, axis=-1, keepdims=True) + 1e-06) * gain
        return (v * COS[yb] + pltpu.roll(v, 64, 1) * SIN[yb]).astype(jnp.bfloat16)

    def project(yb, g):
        rows = NY // 2 * NX * NZ * 32
        low = jnp.dot(H[yb, 0], W[g, 0:2].reshape(rows, 256), preferred_element_type=jnp.float32)
        high = jnp.dot(H[yb, 1], W[g, 2:4].reshape(rows, 256), preferred_element_type=jnp.float32)
        return low + high

    def queries(yb, g):
        out = project(yb, g)
        for h in (0, 1):
            QS[yb, 2 * (g - 1) + h] = turned(out[:, h * HEAD : (h + 1) * HEAD], qg[...], yb)

    def own_queries(g):
        queries(y, g)
        for h in (0, 1):
            QA[4 * y + 2 * (g - 1) + h] = QS[y, 2 * (g - 1) + h]

    def q_send(n, g):
        dy = steps_y[n]
        heads = pl.ds(2 * (g - 1), 2)
        send(QS.at[ym(dy), heads], QA.at[pl.ds(4 * y + 2 * (g - 1), 2)], q_s.at[n, g - 1], q_r.at[n, g - 1], at(dy=dy))

    def q_wait(n, g):
        arrived(QA.at[pl.ds(4 * ym(-steps_y[n]) + 2 * (g - 1), 2)], q_s.at[n, g - 1], q_r.at[n, g - 1])

    def new_kv():
        out = project(y, 0)
        key = turned(out[:, :HEAD], kg[...], y)
        val = out[:, HEAD:].astype(jnp.bfloat16)
        KN[zp] = key
        VN[zp] = val
        nk[...] = key
        nv[...] = val
        send(KN.at[zp], KN.at[zp], kv_s.at[2], kv_r.at[2], pair)
        send(VN.at[zp], VN.at[zp], kv_s.at[3], kv_r.at[3], pair)

    def arrange_keys():
        b = trajectory(y)
        count = counts[b]
        first = jnp.broadcast_to(KN[0, 0:1, :].astype(jnp.float32), (BLOCK, HEAD))

        def put(at_row, on, k, v):
            on = jnp.full((BLOCK, HEAD), on, jnp.int32) > 0
            KM[pl.ds(at_row, BLOCK), :] = jnp.where(on, k.astype(jnp.float32), first).astype(jnp.bfloat16)
            VM[pl.ds(at_row, BLOCK), 0:HEAD] = jnp.where(on, v.astype(jnp.float32), 0.0).astype(jnp.bfloat16)
            VM[pl.ds(at_row, BLOCK), HEAD : 2 * HEAD] = jnp.where(on, 1.0, 0.0).astype(jnp.bfloat16)

        for s in range(SLOTS):
            on = jnp.int32(0)
            for j in range(SLOTS):
                hit = jnp.where(place[b, j] == s, 1, 0) * jnp.where(j < count, 1, 0)
                on = jnp.maximum(on, hit)
            rows = pl.ds(s % 8 * BLOCK, BLOCK)
            put(s * BLOCK, on, KC[s // 8, rows, :], VC[s // 8, rows, :])
        for s in range(2):
            rows = pl.ds(s * BLOCK, BLOCK)
            put(CACHE + s * BLOCK, zp, KN[1 - zp, rows, :], VN[1 - zp, rows, :])
            put(CACHE + TOK + s * BLOCK, jnp.int32(1), KN[zp, rows, :], VN[zp, rows, :])

    def attend(first_head, number):
        def body(n, carry):
            h = first_head + n
            s = lax.dot_general(QA[h], KM[...], (((1,), (1,)), ((), ())), preferred_element_type=jnp.float32)
            s_own = s[:, CACHE + TOK :] + TRI[...]
            s_rest = s[:, : CACHE + TOK]
            top = jnp.maximum(
                jnp.max(s_rest, axis=-1, keepdims=True), jnp.max(s_own, axis=-1, keepdims=True)
            )
            w_rest = jnp.exp2((s_rest - top) * FACTOR).astype(jnp.bfloat16)
            w_own = jnp.exp2((s_own - top) * FACTOR).astype(jnp.bfloat16)
            mixed = jnp.dot(w_rest, VM[: CACHE + TOK], preferred_element_type=jnp.float32) + jnp.dot(
                w_own, VM[CACHE + TOK :], preferred_element_type=jnp.float32
            )
            O[h] = (mixed[:, :HEAD] / mixed[:, HEAD:]).astype(jnp.bfloat16)
            return carry

        lax.fori_loop(0, number, body, 0)
        for n in range(number):
            h = first_head + n
            copy = pltpu.make_async_copy(O.at[h], att.at[:, pl.ds(pl.multiple_of(h * HEAD, HEAD), HEAD)], out_sem.at[h])
            copy.start()
            written.append(copy)

    written = []

    for copy in local[:1]:
        copy.wait()
    a_step(1, 0)
    for copy in local[1:3]:
        copy.wait()
    b_step(0)
    tables(y)
    a_step(1, 1)
    b_step(1)
    send(ck, KC.at[zp], kv_s.at[0], kv_r.at[0], pair)
    send(cv, VC.at[zp], kv_s.at[1], kv_r.at[1], pair)
    row = lax.broadcasted_iota(jnp.int32, (TOK, TOK), 0)
    col = lax.broadcasted_iota(jnp.int32, (TOK, TOK), 1)
    TRI[...] = jnp.where(col <= row, 0.0, NEG)
    a_step(1, 2)
    b_step(2)
    a_step(1, 3)
    tables(ym(1))
    a_step(1, 4)
    local[3].wait()
    a_step(2, 0)
    tables(ym(-1))
    b_step(3)
    for d in (0, 1):
        h_arrived(d, d)
        h_forward(d)
    a_step(1, 5)
    a_step(2, 1)
    b_step(4)
    tables(ym(2))
    a_step(2, 2)
    a_step(1, 6)
    for copy in local[4:]:
        copy.wait()
    h_from_core(y, 0)
    own_queries(1)
    a_step(2, 3)
    b_step(5)
    for d in (0, 1):
        h_arrived(d, 1 - d)
        h_to_core(ym(-1 if d == 0 else 1), 1 + d)
    a_step(2, 4)
    b_step(6)
    new_kv()
    for d in (0, 1):
        h_from_core(ym(-1 if d == 0 else 1), 1 + d)
    queries(ym(1), 1)
    q_send(0, 1)
    a_step(2, 5)
    queries(ym(-1), 1)
    q_send(1, 1)
    arrived(KC.at[1 - zp], kv_s.at[0], kv_r.at[0])
    arrived(VC.at[1 - zp], kv_s.at[1], kv_r.at[1])
    arrived(KN.at[1 - zp], kv_s.at[2], kv_r.at[2])
    arrived(VN.at[1 - zp], kv_s.at[3], kv_r.at[3])
    arrange_keys()
    for d in (0, 1):
        h_far_arrived(d)
        h_to_core(ym(2), 3 + d, half(d))
    attend(4 * y, 2)
    a_step(2, 6)
    queries(ym(1), 2)
    q_send(0, 2)
    queries(ym(-1), 2)
    q_send(1, 2)
    for d in (0, 1):
        h_from_core(ym(2), 3 + d, half(d))
    queries(ym(2), 1)
    q_send(2, 1)
    queries(ym(2), 2)
    q_send(2, 2)
    own_queries(2)
    attend(4 * y + 2, 2)
    for n in (0, 1):
        q_wait(n, 1)
        attend(4 * ym(-steps_y[n]), 2)
    for n in (0, 1):
        q_wait(n, 2)
        attend(4 * ym(-steps_y[n]) + 2, 2)
    for g in (1, 2):
        q_wait(2, g)
        attend(4 * ym(2) + 2 * (g - 1), 2)
    for copy in written:
        copy.wait()
    for copy in sent:
        copy.wait_send()


def on_device(hidden, w_query, key_weight, value_weight, q_gain, key_norm_gain, earlier_keys, earlier_values, counts, place):
    vmem = pl.BlockSpec(memory_space=pltpu.VMEM)
    smem = pl.BlockSpec(memory_space=pltpu.SMEM)
    hbm = pl.BlockSpec(memory_space=pl.ANY)
    bf16, f32 = jnp.bfloat16, jnp.float32
    dma = pltpu.SemaphoreType.DMA

    def both(*shape):
        return [dma(shape), dma(shape)]

    return pl.pallas_call(
        kernel,
        name="prefill",
        out_shape=(
            jax.ShapeDtypeStruct((TOK, 16 * HEAD), bf16),
            jax.ShapeDtypeStruct((TOK, HEAD), bf16),
            jax.ShapeDtypeStruct((TOK, HEAD), bf16),
        ),
        in_specs=[smem, smem, hbm, hbm, hbm, hbm, vmem, vmem, hbm, hbm],
        out_specs=(hbm, vmem, vmem),
        scratch_shapes=[
            pltpu.VMEM((NY, 2, TOK, 2048), bf16),
            pltpu.VMEM((3, NY, NX, NZ, 32, 256), bf16),
            pltpu.VMEM((2, 1024, HEAD), bf16),
            pltpu.VMEM((2, 1024, HEAD), bf16),
            pltpu.VMEM((2, TOK, HEAD), bf16),
            pltpu.VMEM((2, TOK, HEAD), bf16),
            pltpu.VMEM((KEYS, HEAD), bf16),
            pltpu.VMEM((KEYS, 2 * HEAD), bf16),
            pltpu.VMEM((NY, 4, TOK, HEAD), bf16),
            pltpu.VMEM((16, TOK, HEAD), bf16),
            pltpu.VMEM((NY, TOK, HEAD), f32),
            pltpu.VMEM((NY, TOK, HEAD), f32),
            pltpu.VMEM((TOK, TOK), f32),
            pltpu.VMEM((16, TOK, HEAD), bf16),
            dma((7,)),
            dma((16,)),
            *both(3, 4),
            *both(3, 2),
            *both(5),
            *both(4),
            *both(2, 2, 4),
            *both(2, 3, 8),
            *both(4),
            *both(4, 2, 4),
            *both(3, 2),
        ],
        compiler_params=pltpu.CompilerParams(
            collective_id=0, has_side_effects=True, vmem_limit_bytes=52 << 20
        ),
    )(
        counts,
        place,
        hidden,
        w_query,
        key_weight,
        value_weight,
        q_gain.reshape(1, HEAD),
        key_norm_gain.reshape(1, HEAD),
        earlier_keys,
        earlier_values,
    )


def solution(mesh):
    placed = (
        P("ctx", "tp"),
        P("ctx", "tp"),
        P("ctx", "tp"),
        P("ctx", "tp"),
        P(),
        P(),
        P("ctx", "tp"),
        P("ctx", "tp"),
        P(),
        P(),
    )
    return jax.shard_map(
        on_device,
        mesh=mesh,
        in_specs=placed,
        out_specs=(P("ctx", "tp"), P("ctx", "tp"), P("ctx", "tp")),
        check_vma=False,
    )
```

```python
import functools
import math

import jax
import jax.numpy as jnp
from jax import lax
from jax.experimental import pallas as pl
from jax.experimental.pallas import tpu as pltpu
from jax.sharding import PartitionSpec as P

MESH = pl.DeviceIdType.MESH
HEAD = 128
BLOCK = 128
TOK = 256
NY, NX, NZ = 4, 4, 8
SLOTS = 16
CACHE = SLOTS * BLOCK
KEYS = CACHE + 2 * TOK
FACTOR = HEAD**-0.5 * math.log2(math.e)
NEG = -1e30


def kernel(
    counts_in, place_in, hid, wq, kw, vw, qg_in, kg_in, ck, cv,
    att, nk, nv,
    H, W, W0, KVW, KC, VC, NEW, PB, KM, VM, QS, QA, COS, SIN, TRI, O, counts, place, qg, kg,
    local_sem, out_sem,
    p0_s, p0_r, h_s, h_r, c_s, c_r, kv_s, kv_r, za_s, za_r, xa_s, xa_r, xb_s, xb_r, zb_s, zb_r, q_s, q_r,
):
    i = lax.axis_index("ctx")
    c = lax.axis_index("tp")
    y, x, z = i // (NX * NZ), (i // NZ) % NX, i % NZ
    zp = z % 2
    kind = y % 2
    toward = 1 - 2 * kind
    sent = []

    def ym(k):
        return (y + k + NY) % NY

    def xm(k):
        return (x + k + NX) % NX

    def zm(k):
        return (z + k + NZ) % NZ

    def at(dy=0, dx=0, dz=0):
        return (ym(dy) * (NX * NZ) + xm(dx) * NZ + zm(dz), c)

    other_core = (i, 1 - c)
    pair = (i + 1 - 2 * zp, c)

    def send(src, dst, s, r, device):
        copy = pltpu.make_async_remote_copy(
            src_ref=src, dst_ref=dst, send_sem=s, recv_sem=r, device_id=device, device_id_type=MESH
        )
        copy.start()
        sent.append(copy)

    def arrived(dst, s, r):
        pltpu.make_async_remote_copy(
            src_ref=dst, dst_ref=dst, send_sem=s, recv_sem=r, device_id=other_core, device_id_type=MESH
        ).wait_recv()

    local = {}

    def bring(name, src, dst):
        copy = pltpu.make_async_copy(src, dst, local_sem.at[len(local)])
        copy.start()
        local[name] = copy

    def columns(yb, g):
        return pl.ds(pl.multiple_of(yb * 512 + (g - 1) * 256, 256), 256)

    bring("kw", kw, KVW.at[0])
    bring("vw", vw, KVW.at[1])
    bring("w1", wq.at[:, columns(y, 1)], W.at[0, y, x, z])
    bring("w2", wq.at[:, columns(y, 2)], W.at[1, y, x, z])
    bring("counts", counts_in, counts)
    bring("place", place_in, place)
    bring("qg", qg_in, qg)
    bring("kg", kg_in, kg)
    bring("hid", hid, H.at[y, c])
    bring("ck", ck, KC.at[zp])
    bring("cv", cv, VC.at[zp])

    barrier = pltpu.get_barrier_semaphore()
    for device in (at(dy=1), at(dy=-1), at(dy=2), at(dx=1), at(dx=-1), at(dz=1), at(dz=-1), other_core):
        pl.semaphore_signal(barrier, inc=1, device_id=device, device_id_type=MESH)
    pl.semaphore_wait(barrier, 8)

    steps_y = (1, -1, 2)

    def p0_queries(g):
        for n, dy in enumerate(steps_y):
            send(wq.at[:, columns(ym(dy), g)], W.at[g - 1, y, x, z], p0_s.at[n, g], p0_r.at[n, g], at(dy=dy))

    def p0_kv():
        for n, dy in enumerate(steps_y):
            send(KVW.at[ym(dy) % 2], W0.at[y, x, z], p0_s.at[n, 0], p0_r.at[n, 0], at(dy=dy))

    p0_queries(1)
    local["kw"].wait()
    local["vw"].wait()
    p0_kv()
    p0_queries(2)

    def own_rows(g):
        for n, dy in enumerate(steps_y):
            ref = W0.at[ym(-dy), x, z] if g == 0 else W.at[g - 1, ym(-dy), x, z]
            arrived(ref, p0_s.at[n, g], p0_r.at[n, g])

    def half(n):
        return pl.ds(128 * n, 128)

    def quarter(n):
        return pl.ds(64 * n, 64)

    for n in (0, 1):
        send(hid.at[half(n)], H.at[y, c, half(n)], h_s.at[0, n], h_r.at[0, n], at(dy=1))
        send(hid.at[half(1 - n)], H.at[y, c, half(1 - n)], h_s.at[1, 1 - n], h_r.at[1, 1 - n], at(dy=-1))
    send(hid, H.at[y, c], c_s.at[0], c_r.at[0], other_core)

    def side(d):
        return ym(-1 if d == 0 else 1)

    def h_arrived(d, n):
        arrived(H.at[side(d), c, half(n)], h_s.at[d, n], h_r.at[d, n])

    def h_forward(n):
        for d in (0, 1):
            ref = H.at[side(d), c, quarter(2 * d + n)]
            send(ref, ref, h_s.at[2, 2 * d + n], h_r.at[2, 2 * d + n], at(dy=1 if d == 0 else -1))

    def h_far(n):
        for d in (0, 1):
            ref = H.at[ym(2), c, quarter(2 * d + n)]
            arrived(ref, h_s.at[2, 2 * d + n], h_r.at[2, 2 * d + n])
            send(ref, ref, c_s.at[3 + 2 * d + n], c_r.at[3 + 2 * d + n], other_core)

    def h_far_from_core():
        for n in range(4):
            arrived(H.at[ym(2), 1 - c, quarter(n)], c_s.at[3 + n], c_r.at[3 + n])

    def h_to_core(d):
        send(H.at[side(d), c], H.at[side(d), c], c_s.at[1 + d], c_r.at[1 + d], other_core)

    def h_from_core(yb, slot):
        arrived(H.at[yb, 1 - c], c_s.at[slot], c_r.at[slot])

    def order(j):
        return zm((0, -1, 1, -2, 2, -3, 3, 4)[j])

    def a_block(g, xx, zz, hop=1, d=0):
        ref = W0 if g == 0 else W.at[g - 1]
        if hop == 4:
            return ref.at[pl.ds(2 * d, 2), xx, zz]
        return ref.at[:, xx, zz]

    def a_zsend(g, d, hop):
        sign = 1 - 2 * d
        ref = a_block(g, x, zm(-sign * (hop - 1)), hop, d)
        send(ref, ref, za_s.at[g - 1, d, hop - 1], za_r.at[g - 1, d, hop - 1], at(dz=sign))

    def a_zwait(g, d, hop):
        sign = 1 - 2 * d
        arrived(a_block(g, x, zm(-sign * hop), hop, d), za_s.at[g - 1, d, hop - 1], za_r.at[g - 1, d, hop - 1])

    def a_xsend(g, *blocks):
        for j in blocks:
            for d in (0, 1):
                ref = a_block(g, x, order(j))
                send(ref, ref, xa_s.at[g - 1, d, j], xa_r.at[g - 1, d, j], at(dx=1 - 2 * d))

    def a_xwait(g, d, j):
        arrived(a_block(g, xm(2 * d - 1), order(j)), xa_s.at[g - 1, d, j], xa_r.at[g - 1, d, j])

    def a_xforward(g, *blocks):
        for j in blocks:
            d = j % 2
            a_xwait(g, d, j)
            ref = a_block(g, xm(2 * d - 1), order(j))
            send(ref, ref, xa_s.at[g - 1, 2, j], xa_r.at[g - 1, 2, j], at(dx=1 - 2 * d))

    def a_z(g, n):
        if n == 0:
            own_rows(g)
        for d in (0, 1):
            if n:
                a_zwait(g, d, n)
            if n < 4:
                a_zsend(g, d, n + 1)

    def a_end(g):
        for j in range(8):
            a_xwait(g, 1 - j % 2, j)
            arrived(a_block(g, xm(2), order(j)), xa_s.at[g - 1, 2, j], xa_r.at[g - 1, 2, j])

    far = (0, -1, 1, 2)

    def b_zsend(n, hop):
        for d in (0, 1):
            sign = 1 - 2 * d
            ref = a_block(0, xm(far[n]), zm(-sign * (hop - 1)), hop, d)
            send(ref, ref, zb_s.at[n, d, hop - 1], zb_r.at[n, d, hop - 1], at(dz=sign))

    def b_zwait(n, hop):
        for d in (0, 1):
            sign = 1 - 2 * d
            arrived(a_block(0, xm(far[n]), zm(-sign * hop), hop, d), zb_s.at[n, d, hop - 1], zb_r.at[n, d, hop - 1])

    def b_step(n):
        if n == 0:
            own_rows(0)
            for d in (0, 1):
                ref = a_block(0, x, z)
                send(ref, ref, xb_s.at[d], xb_r.at[d], at(dx=1 - 2 * d))
            b_zsend(0, 1)
        elif n == 1:
            for d in (0, 1):
                arrived(a_block(0, xm(2 * d - 1), z), xb_s.at[d], xb_r.at[d])
                ref = a_block(0, xm(2 * d - 1), z, 4, d)
                send(ref, ref, xb_s.at[2 + d], xb_r.at[2 + d], at(dx=1 - 2 * d))
            b_zsend(1, 1)
            b_zsend(2, 1)
        elif n == 2:
            for d in (0, 1):
                arrived(a_block(0, xm(2), z, 4, d), xb_s.at[2 + d], xb_r.at[2 + d])
            b_zsend(3, 1)
        elif n <= 5:
            for m in range(4):
                b_zwait(m, n - 2)
                b_zsend(m, n - 1)
        else:
            for m in range(4):
                b_zwait(m, 4)

    def trajectory(yb):
        return (yb * (NX * NZ) + x * NZ + z) // 2

    def tables(yb):
        lane = lax.broadcasted_iota(jnp.int32, (TOK, HEAD), 1)
        freq = jnp.exp((lane % 64).astype(jnp.float32) * (-2.0 / HEAD) * math.log(1000000.0))
        start = counts[trajectory(yb)] * BLOCK + zp * TOK
        pos = (start + lax.broadcasted_iota(jnp.int32, (TOK, HEAD), 0)).astype(jnp.float32)
        angle = pos * freq
        COS[yb] = jnp.cos(angle)
        SIN[yb] = jnp.where(lane < 64, -1.0, 1.0) * jnp.sin(angle)

    def turned(v, gain, yb):
        v = v * lax.rsqrt(jnp.mean(v * v, axis=-1, keepdims=True) + 1e-06) * gain
        return (v * COS[yb] + pltpu.roll(v, 64, 1) * SIN[yb]).astype(jnp.bfloat16)

    def project(yb, w):
        rows, width = NY // 2 * NX * NZ * 32, w.shape[-1]
        low = jnp.dot(H[yb, 0], w[0:2].reshape(rows, width), preferred_element_type=jnp.float32)
        high = jnp.dot(H[yb, 1], w[2:4].reshape(rows, width), preferred_element_type=jnp.float32)
        return low + high

    def queries(yb, g):
        out = project(yb, W.at[g - 1])
        for h in (0, 1):
            QS[yb, 2 * (g - 1) + h] = turned(out[:, h * HEAD : (h + 1) * HEAD], qg[...], yb)

    def own_queries(g):
        queries(y, g)
        for h in (0, 1):
            QA[4 * y + 2 * (g - 1) + h] = QS[y, 2 * (g - 1) + h]

    def q_send(n, g):
        dy = steps_y[n]
        heads = pl.ds(2 * (g - 1), 2)
        send(QS.at[ym(dy), heads], QA.at[pl.ds(4 * y + 2 * (g - 1), 2)], q_s.at[n, g - 1], q_r.at[n, g - 1], at(dy=dy))

    def q_wait(n, g):
        arrived(QA.at[pl.ds(4 * ym(-steps_y[n]) + 2 * (g - 1), 2)], q_s.at[n, g - 1], q_r.at[n, g - 1])

    def fresh(yb):
        out = project(yb, W0)
        keys = jnp.full((TOK, HEAD), kind, jnp.int32) == 0
        return jnp.where(keys, turned(out, kg[...], yb).astype(jnp.float32), out).astype(jnp.bfloat16)

    def arrange_keys():
        b = trajectory(y)
        mine = lax.broadcasted_iota(jnp.int32, (SLOTS, 64), 1) == b
        slot_order = jnp.sum(jnp.where(mine, place[...].astype(jnp.float32), 0.0), axis=1, keepdims=True)
        used = lax.broadcasted_iota(jnp.int32, (SLOTS, 1), 0) < counts[b]
        first = jnp.broadcast_to(NEW[0, 0, 0:1, :].astype(jnp.float32), (BLOCK, HEAD))

        def put(at_row, on, k, v):
            KM[pl.ds(at_row, BLOCK), :] = jnp.where(on, k.astype(jnp.float32), first).astype(jnp.bfloat16)
            VM[pl.ds(at_row, BLOCK), 0:HEAD] = jnp.where(on, v.astype(jnp.float32), 0.0).astype(jnp.bfloat16)
            VM[pl.ds(at_row, BLOCK), HEAD : 2 * HEAD] = jnp.where(on, 1.0, 0.0).astype(jnp.bfloat16)

        for s in range(SLOTS):
            hit = jnp.where(used, jnp.where(slot_order == s, 1.0, 0.0), 0.0)
            on = jnp.broadcast_to(jnp.max(hit, axis=0, keepdims=True), (BLOCK, HEAD)) > 0.5
            rows = pl.ds(s % 8 * BLOCK, BLOCK)
            put(s * BLOCK, on, KC[s // 8, rows, :], VC[s // 8, rows, :])
        for s in range(2):
            rows = pl.ds(s * BLOCK, BLOCK)
            seen = jnp.full((BLOCK, HEAD), zp, jnp.int32) > 0
            put(CACHE + s * BLOCK, seen, NEW[0, 1 - zp, rows, :], NEW[1, 1 - zp, rows, :])
            put(CACHE + TOK + s * BLOCK, seen | True, NEW[0, zp, rows, :], NEW[1, zp, rows, :])

    def attend(*heads):
        scores = []
        for h in heads:
            s = lax.dot_general(QA[h], KM[...], (((1,), (1,)), ((), ())), preferred_element_type=jnp.float32)
            s_own = s[:, CACHE + TOK :] + TRI[...]
            s_rest = s[:, : CACHE + TOK]
            top = jnp.maximum(jnp.max(s_rest, axis=-1, keepdims=True), jnp.max(s_own, axis=-1, keepdims=True))
            scores.append((s_rest, s_own, top))
        for h, (s_rest, s_own, top) in zip(heads, scores):
            w_rest = jnp.exp2((s_rest - top) * FACTOR).astype(jnp.bfloat16)
            w_own = jnp.exp2((s_own - top) * FACTOR).astype(jnp.bfloat16)
            mixed = jnp.dot(w_rest, VM[: CACHE + TOK], preferred_element_type=jnp.float32) + jnp.dot(
                w_own, VM[CACHE + TOK :], preferred_element_type=jnp.float32
            )
            O[h] = (mixed[:, :HEAD] / mixed[:, HEAD:]).astype(jnp.bfloat16)
        for h in heads:
            written(h).start()

    def written(h):
        return pltpu.make_async_copy(O.at[h], att.at[:, pl.ds(pl.multiple_of(h * HEAD, HEAD), HEAD)], out_sem.at[h])

    local["w1"].wait()
    a_z(1, 0)
    a_xsend(1, 0)
    local["w2"].wait()
    a_z(2, 0)
    W0[y, x, z] = KVW[kind]
    b_step(0)
    for name in ("counts", "place", "qg", "kg"):
        local[name].wait()
    a_z(1, 1)
    a_xsend(1, 1, 2)
    a_z(2, 1)
    a_xforward(1, 0)
    b_step(1)
    tables(y)
    a_z(1, 2)
    a_xsend(1, 3, 4)
    a_z(2, 2)
    a_xforward(1, 1, 2)
    b_step(2)
    tables(ym(1))
    a_z(1, 3)
    a_xsend(1, 5, 6)
    a_z(2, 3)
    a_xforward(1, 3, 4)
    b_step(3)
    tables(ym(-1))
    a_z(1, 4)
    a_xsend(1, 7)
    a_z(2, 4)
    b_step(4)
    a_xforward(1, 5, 6)
    a_xsend(2, 0, 1, 2, 3)
    tables(ym(2))
    for d in (0, 1):
        h_arrived(d, d)
    b_step(5)
    a_xforward(1, 7)
    a_xsend(2, 4, 5, 6, 7)
    row = lax.broadcasted_iota(jnp.int32, (TOK, TOK), 0)
    col = lax.broadcasted_iota(jnp.int32, (TOK, TOK), 1)
    TRI[...] = jnp.where(col <= row, 0.0, NEG)
    send(ck, KC.at[zp], kv_s.at[0], kv_r.at[0], pair)
    send(cv, VC.at[zp], kv_s.at[1], kv_r.at[1], pair)
    b_step(6)
    for d in (0, 1):
        h_arrived(d, 1 - d)
        h_to_core(d)
    h_forward(0)
    a_end(1)
    for name in ("hid", "ck", "cv"):
        local[name].wait()
    h_from_core(y, 0)
    own_queries(1)
    NEW[kind, zp] = fresh(y)
    for d in (0, 1):
        h_from_core(side(d), 1 + d)
    PB[...] = fresh(ym(toward))
    send(PB, NEW.at[kind, zp], kv_s.at[4], kv_r.at[4], at(dy=toward))
    a_xforward(2, 0, 1)
    queries(ym(1), 1)
    q_send(0, 1)
    a_xforward(2, 2, 3)
    queries(ym(-1), 1)
    q_send(1, 1)
    h_forward(1)
    a_xforward(2, 4, 5)
    arrived(NEW.at[1 - kind, zp], kv_s.at[4], kv_r.at[4])
    for n in (0, 1):
        send(NEW.at[n, zp], NEW.at[n, zp], kv_s.at[2 + n], kv_r.at[2 + n], pair)
    nk[...] = NEW[0, zp]
    nv[...] = NEW[1, zp]
    a_xforward(2, 6, 7)
    h_far(0)
    arrived(KC.at[1 - zp], kv_s.at[0], kv_r.at[0])
    arrived(VC.at[1 - zp], kv_s.at[1], kv_r.at[1])
    for n in (0, 1):
        arrived(NEW.at[n, 1 - zp], kv_s.at[2 + n], kv_r.at[2 + n])
    arrange_keys()
    q_wait(0, 1)
    attend(4 * y, 4 * y + 1, 4 * ym(-1), 4 * ym(-1) + 1)
    h_far(1)
    a_end(2)
    queries(ym(1), 2)
    q_send(0, 2)
    queries(ym(-1), 2)
    q_send(1, 2)
    h_far_from_core()
    queries(ym(2), 1)
    q_send(2, 1)
    queries(ym(2), 2)
    q_send(2, 2)
    own_queries(2)
    q_wait(1, 1)

    def four(n, carry):
        @pl.when(n == 1)
        def _():
            q_wait(0, 2)
            q_wait(1, 2)

        @pl.when(n == 2)
        def _():
            q_wait(2, 1)
            q_wait(2, 2)

        a = 4 * ((y + 1 + 2 * n - 3 * (n // 2)) % NY) + 2 * (n % 2)
        b = 4 * ((y + n) % NY) + 2
        attend(a, a + 1, b, b + 1)
        return carry

    lax.fori_loop(0, 3, four, 0)
    for h in range(4 * NY):
        written(h).wait()
    for copy in sent:
        copy.wait_send()


def on_device(hidden, w_query, key_weight, value_weight, q_gain, key_norm_gain, earlier_keys, earlier_values, counts, place):
    vmem = pl.BlockSpec(memory_space=pltpu.VMEM)
    hbm = pl.BlockSpec(memory_space=pltpu.HBM)
    bf16, f32 = jnp.bfloat16, jnp.float32
    dma = pltpu.SemaphoreType.DMA

    def both(*shape):
        return [dma(shape), dma(shape)]

    return pl.pallas_call(
        kernel,
        name="prefill",
        out_shape=(
            jax.ShapeDtypeStruct((TOK, 16 * HEAD), bf16),
            jax.ShapeDtypeStruct((TOK, HEAD), bf16),
            jax.ShapeDtypeStruct((TOK, HEAD), bf16),
        ),
        in_specs=[hbm] * 10,
        out_specs=(hbm, vmem, vmem),
        scratch_shapes=[
            pltpu.VMEM((NY, 2, TOK, 2048), bf16),
            pltpu.VMEM((2, NY, NX, NZ, 32, 256), bf16),
            pltpu.VMEM((NY, NX, NZ, 32, HEAD), bf16),
            pltpu.VMEM((2, 32, HEAD), bf16),
            pltpu.VMEM((2, 1024, HEAD), bf16),
            pltpu.VMEM((2, 1024, HEAD), bf16),
            pltpu.VMEM((2, 2, TOK, HEAD), bf16),
            pltpu.VMEM((TOK, HEAD), bf16),
            pltpu.VMEM((KEYS, HEAD), bf16),
            pltpu.VMEM((KEYS, 2 * HEAD), bf16),
            pltpu.VMEM((NY, 4, TOK, HEAD), bf16),
            pltpu.VMEM((16, TOK, HEAD), bf16),
            pltpu.VMEM((NY, TOK, HEAD), f32),
            pltpu.VMEM((NY, TOK, HEAD), f32),
            pltpu.VMEM((TOK, TOK), f32),
            pltpu.VMEM((16, TOK, HEAD), bf16),
            pltpu.SMEM((64,), jnp.int32),
            pltpu.VMEM((SLOTS, 64), jnp.int32),
            pltpu.VMEM((1, HEAD), f32),
            pltpu.VMEM((1, HEAD), f32),
            dma((11,)),
            dma((16,)),
            *both(3, 3),
            *both(3, 4),
            *both(7),
            *both(5),
            *both(2, 2, 4),
            *both(2, 3, 8),
            *both(4),
            *both(4, 2, 4),
            *both(3, 2),
        ],
        compiler_params=pltpu.CompilerParams(
            collective_id=0, has_side_effects=True, vmem_limit_bytes=52 << 20
        ),
    )(
        *(
            pltpu.with_memory_space_constraint(a, pltpu.HBM)
            for a in (
                counts,
                place.T,
                hidden,
                w_query,
                key_weight,
                value_weight,
                q_gain.reshape(1, HEAD),
                key_norm_gain.reshape(1, HEAD),
                earlier_keys,
                earlier_values,
            )
        )
    )


def solution(mesh):
    placed = (
        P("ctx", "tp"),
        P("ctx", "tp"),
        P("ctx", "tp"),
        P("ctx", "tp"),
        P(),
        P(),
        P("ctx", "tp"),
        P("ctx", "tp"),
        P(),
        P(),
    )
    return jax.shard_map(
        on_device,
        mesh=mesh,
        in_specs=placed,
        out_specs=(P("ctx", "tp"), P("ctx", "tp"), P("ctx", "tp")),
        check_vma=False,
    )
```

```python
import functools
import math

import jax
import jax.numpy as jnp
from jax import lax
from jax.experimental import pallas as pl
from jax.experimental.pallas import tpu as pltpu
from jax.sharding import PartitionSpec as P

MESH = pl.DeviceIdType.MESH
HEAD = 128
BLOCK = 128
TOK = 256
NY, NX, NZ = 4, 4, 8
SLOTS = 16
CACHE = SLOTS * BLOCK
KEYS = CACHE + 2 * TOK
FACTOR = HEAD**-0.5 * math.log2(math.e)
NEG = -1e30


def kernel(
    counts_in, place_in, hid, wq, kw, vw, qg_in, kg_in, ck, cv,
    att, nk, nv,
    H, W, W0, KVW, KC, VC, NEW, PB, KM, VM, QS, QA, COS, SIN, TRI, O, counts, place, qg, kg,
    local_sem, out_sem,
    p0_s, p0_r, h_s, h_r, c_s, c_r, kv_s, kv_r, za_s, za_r, xa_s, xa_r, xb_s, xb_r, zb_s, zb_r, q_s, q_r,
):
    i = lax.axis_index("ctx")
    c = lax.axis_index("tp")
    y, x, z = i // (NX * NZ), (i // NZ) % NX, i % NZ
    zp = z % 2
    kind = y % 2
    toward = 1 - 2 * kind
    sent = []

    def ym(k):
        return (y + k + NY) % NY

    def xm(k):
        return (x + k + NX) % NX

    def zm(k):
        return (z + k + NZ) % NZ

    def at(dy=0, dx=0, dz=0):
        return (ym(dy) * (NX * NZ) + xm(dx) * NZ + zm(dz), c)

    other_core = (i, 1 - c)
    pair = (i + 1 - 2 * zp, c)

    def send(src, dst, s, r, device):
        copy = pltpu.make_async_remote_copy(
            src_ref=src, dst_ref=dst, send_sem=s, recv_sem=r, device_id=device, device_id_type=MESH
        )
        copy.start()
        sent.append(copy)

    def arrived(dst, s, r):
        pltpu.make_async_remote_copy(
            src_ref=dst, dst_ref=dst, send_sem=s, recv_sem=r, device_id=other_core, device_id_type=MESH
        ).wait_recv()

    local = {}

    def bring(name, src, dst):
        copy = pltpu.make_async_copy(src, dst, local_sem.at[len(local)])
        copy.start()
        local[name] = copy

    def columns(yb, g):
        return pl.ds(pl.multiple_of(yb * 512 + (g - 1) * 256, 256), 256)

    bring("kw", kw, KVW.at[0])
    bring("vw", vw, KVW.at[1])
    bring("w1", wq.at[:, columns(y, 1)], W.at[0, y, x, z])
    bring("w2", wq.at[:, columns(y, 2)], W.at[1, y, x, z])
    bring("counts", counts_in, counts)
    bring("place", place_in, place)
    bring("qg", qg_in, qg)
    bring("kg", kg_in, kg)
    bring("hid", hid, H.at[y, c])
    bring("ck", ck, KC.at[zp])
    bring("cv", cv, VC.at[zp])

    barrier = pltpu.get_barrier_semaphore()
    for device in (at(dy=1), at(dy=-1), at(dy=2), at(dx=1), at(dx=-1), at(dz=1), at(dz=-1), other_core):
        pl.semaphore_signal(barrier, inc=1, device_id=device, device_id_type=MESH)
    pl.semaphore_wait(barrier, 8)

    steps_y = (1, -1, 2)

    def p0_queries(g):
        for n, dy in enumerate(steps_y):
            send(wq.at[:, columns(ym(dy), g)], W.at[g - 1, y, x, z], p0_s.at[n, g], p0_r.at[n, g], at(dy=dy))

    def p0_kv():
        for n, dy in enumerate(steps_y):
            send(KVW.at[ym(dy) % 2], W0.at[y, x, z], p0_s.at[n, 0], p0_r.at[n, 0], at(dy=dy))

    p0_queries(1)
    local["kw"].wait()
    local["vw"].wait()
    p0_kv()
    p0_queries(2)

    def own_rows(g):
        for n, dy in enumerate(steps_y):
            ref = W0.at[ym(-dy), x, z] if g == 0 else W.at[g - 1, ym(-dy), x, z]
            arrived(ref, p0_s.at[n, g], p0_r.at[n, g])

    def half(n):
        return pl.ds(128 * n, 128)

    def quarter(n):
        return pl.ds(64 * n, 64)

    for n in (0, 1):
        send(hid.at[half(n)], H.at[y, c, half(n)], h_s.at[0, n], h_r.at[0, n], at(dy=1))
        send(hid.at[half(1 - n)], H.at[y, c, half(1 - n)], h_s.at[1, 1 - n], h_r.at[1, 1 - n], at(dy=-1))
    send(hid, H.at[y, c], c_s.at[0], c_r.at[0], other_core)

    def side(d):
        return ym(-1 if d == 0 else 1)

    def h_arrived(d, n):
        arrived(H.at[side(d), c, half(n)], h_s.at[d, n], h_r.at[d, n])

    def h_forward(n):
        for d in (0, 1):
            ref = H.at[side(d), c, quarter(2 * d + n)]
            send(ref, ref, h_s.at[2, 2 * d + n], h_r.at[2, 2 * d + n], at(dy=1 if d == 0 else -1))

    def h_far(n):
        for d in (0, 1):
            ref = H.at[ym(2), c, quarter(2 * d + n)]
            arrived(ref, h_s.at[2, 2 * d + n], h_r.at[2, 2 * d + n])
            send(ref, ref, c_s.at[3 + 2 * d + n], c_r.at[3 + 2 * d + n], other_core)

    def h_far_from_core():
        for n in range(4):
            arrived(H.at[ym(2), 1 - c, quarter(n)], c_s.at[3 + n], c_r.at[3 + n])

    def h_to_core(d):
        send(H.at[side(d), c], H.at[side(d), c], c_s.at[1 + d], c_r.at[1 + d], other_core)

    def h_from_core(yb, slot):
        arrived(H.at[yb, 1 - c], c_s.at[slot], c_r.at[slot])

    def order(j):
        return zm((0, -1, 1, -2, 2, -3, 3, 4)[j])

    def a_block(g, xx, zz, hop=1, d=0):
        ref = W0 if g == 0 else W.at[g - 1]
        if hop == 4:
            return ref.at[pl.ds(2 * d, 2), xx, zz]
        return ref.at[:, xx, zz]

    def a_zsend(g, d, hop):
        sign = 1 - 2 * d
        ref = a_block(g, x, zm(-sign * (hop - 1)), hop, d)
        send(ref, ref, za_s.at[g - 1, d, hop - 1], za_r.at[g - 1, d, hop - 1], at(dz=sign))

    def a_zwait(g, d, hop):
        sign = 1 - 2 * d
        arrived(a_block(g, x, zm(-sign * hop), hop, d), za_s.at[g - 1, d, hop - 1], za_r.at[g - 1, d, hop - 1])

    def a_xsend(g, *blocks):
        for j in blocks:
            for d in (0, 1):
                ref = a_block(g, x, order(j))
                send(ref, ref, xa_s.at[g - 1, d, j], xa_r.at[g - 1, d, j], at(dx=1 - 2 * d))

    def a_xwait(g, d, j):
        arrived(a_block(g, xm(2 * d - 1), order(j)), xa_s.at[g - 1, d, j], xa_r.at[g - 1, d, j])

    def a_xforward(g, *blocks):
        for j in blocks:
            d = j % 2
            a_xwait(g, d, j)
            ref = a_block(g, xm(2 * d - 1), order(j))
            send(ref, ref, xa_s.at[g - 1, 2, j], xa_r.at[g - 1, 2, j], at(dx=1 - 2 * d))

    def a_z(g, n):
        if n == 0:
            own_rows(g)
        for d in (0, 1):
            if n:
                a_zwait(g, d, n)
            if n < 4:
                a_zsend(g, d, n + 1)

    def a_end(g):
        for j in range(8):
            a_xwait(g, 1 - j % 2, j)
            arrived(a_block(g, xm(2), order(j)), xa_s.at[g - 1, 2, j], xa_r.at[g - 1, 2, j])

    far = (0, -1, 1, 2)

    def b_zsend(n, hop):
        for d in (0, 1):
            sign = 1 - 2 * d
            ref = a_block(0, xm(far[n]), zm(-sign * (hop - 1)), hop, d)
            send(ref, ref, zb_s.at[n, d, hop - 1], zb_r.at[n, d, hop - 1], at(dz=sign))

    def b_zwait(n, hop):
        for d in (0, 1):
            sign = 1 - 2 * d
            arrived(a_block(0, xm(far[n]), zm(-sign * hop), hop, d), zb_s.at[n, d, hop - 1], zb_r.at[n, d, hop - 1])

    def b_step(n):
        if n == 0:
            own_rows(0)
            for d in (0, 1):
                ref = a_block(0, x, z)
                send(ref, ref, xb_s.at[d], xb_r.at[d], at(dx=1 - 2 * d))
            b_zsend(0, 1)
        elif n == 1:
            for d in (0, 1):
                arrived(a_block(0, xm(2 * d - 1), z), xb_s.at[d], xb_r.at[d])
                ref = a_block(0, xm(2 * d - 1), z, 4, d)
                send(ref, ref, xb_s.at[2 + d], xb_r.at[2 + d], at(dx=1 - 2 * d))
            b_zsend(1, 1)
            b_zsend(2, 1)
        elif n == 2:
            for d in (0, 1):
                arrived(a_block(0, xm(2), z, 4, d), xb_s.at[2 + d], xb_r.at[2 + d])
            b_zsend(3, 1)
        elif n <= 5:
            for m in range(4):
                b_zwait(m, n - 2)
                b_zsend(m, n - 1)
        else:
            for m in range(4):
                b_zwait(m, 4)

    def trajectory(yb):
        return (yb * (NX * NZ) + x * NZ + z) // 2

    def tables(yb):
        lane = lax.broadcasted_iota(jnp.int32, (TOK, HEAD), 1)
        freq = jnp.exp((lane % 64).astype(jnp.float32) * (-2.0 / HEAD) * math.log(1000000.0))
        start = counts[trajectory(yb)] * BLOCK + zp * TOK
        pos = (start + lax.broadcasted_iota(jnp.int32, (TOK, HEAD), 0)).astype(jnp.float32)
        angle = pos * freq
        COS[yb] = jnp.cos(angle)
        SIN[yb] = jnp.where(lane < 64, -1.0, 1.0) * jnp.sin(angle)

    def turned(v, gain, yb):
        v = v * lax.rsqrt(jnp.mean(v * v, axis=-1, keepdims=True) + 1e-06) * gain
        return (v * COS[yb] + pltpu.roll(v, 64, 1) * SIN[yb]).astype(jnp.bfloat16)

    def project(yb, w):
        rows, width = NY // 2 * NX * NZ * 32, w.shape[-1]
        low = jnp.dot(H[yb, 0], w[0:2].reshape(rows, width), preferred_element_type=jnp.float32)
        high = jnp.dot(H[yb, 1], w[2:4].reshape(rows, width), preferred_element_type=jnp.float32)
        return low + high

    def queries(yb, g):
        out = project(yb, W.at[g - 1])
        for h in (0, 1):
            QS[yb, 2 * (g - 1) + h] = turned(out[:, h * HEAD : (h + 1) * HEAD], qg[...], yb)

    def own_queries(g):
        queries(y, g)
        for h in (0, 1):
            QA[4 * y + 2 * (g - 1) + h] = QS[y, 2 * (g - 1) + h]

    def q_send(n, g):
        dy = steps_y[n]
        heads = pl.ds(2 * (g - 1), 2)
        send(QS.at[ym(dy), heads], QA.at[pl.ds(4 * y + 2 * (g - 1), 2)], q_s.at[n, g - 1], q_r.at[n, g - 1], at(dy=dy))

    def q_wait(n, g):
        arrived(QA.at[pl.ds(4 * ym(-steps_y[n]) + 2 * (g - 1), 2)], q_s.at[n, g - 1], q_r.at[n, g - 1])

    def fresh(yb):
        out = project(yb, W0)
        keys = jnp.full((TOK, HEAD), kind, jnp.int32) == 0
        return jnp.where(keys, turned(out, kg[...], yb).astype(jnp.float32), out).astype(jnp.bfloat16)

    def arrange_keys():
        b = trajectory(y)
        mine = lax.broadcasted_iota(jnp.int32, (SLOTS, 64), 1) == b
        slot_order = jnp.sum(jnp.where(mine, place[...].astype(jnp.float32), 0.0), axis=1, keepdims=True)
        used = lax.broadcasted_iota(jnp.int32, (SLOTS, 1), 0) < counts[b]
        first = jnp.broadcast_to(NEW[0, 0, 0:1, :].astype(jnp.float32), (BLOCK, HEAD))

        def put(at_row, on, k, v):
            KM[pl.ds(at_row, BLOCK), :] = jnp.where(on, k.astype(jnp.float32), first).astype(jnp.bfloat16)
            VM[pl.ds(at_row, BLOCK), 0:HEAD] = jnp.where(on, v.astype(jnp.float32), 0.0).astype(jnp.bfloat16)
            VM[pl.ds(at_row, BLOCK), HEAD : 2 * HEAD] = jnp.where(on, 1.0, 0.0).astype(jnp.bfloat16)

        for s in range(SLOTS):
            hit = jnp.where(used, jnp.where(slot_order == s, 1.0, 0.0), 0.0)
            on = jnp.broadcast_to(jnp.max(hit, axis=0, keepdims=True), (BLOCK, HEAD)) > 0.5
            rows = pl.ds(s % 8 * BLOCK, BLOCK)
            put(s * BLOCK, on, KC[s // 8, rows, :], VC[s // 8, rows, :])
        for s in range(2):
            rows = pl.ds(s * BLOCK, BLOCK)
            seen = jnp.full((BLOCK, HEAD), zp, jnp.int32) > 0
            put(CACHE + s * BLOCK, seen, NEW[0, 1 - zp, rows, :], NEW[1, 1 - zp, rows, :])
            put(CACHE + TOK + s * BLOCK, seen | True, NEW[0, zp, rows, :], NEW[1, zp, rows, :])

    def attend(*heads):
        scores = []
        for h in heads:
            s = lax.dot_general(QA[h], KM[...], (((1,), (1,)), ((), ())), preferred_element_type=jnp.float32)
            s_own = s[:, CACHE + TOK :] + TRI[...]
            s_rest = s[:, : CACHE + TOK]
            top = jnp.maximum(jnp.max(s_rest, axis=-1, keepdims=True), jnp.max(s_own, axis=-1, keepdims=True))
            scores.append((s_rest, s_own, top))
        for h, (s_rest, s_own, top) in zip(heads, scores):
            w_rest = jnp.exp2((s_rest - top) * FACTOR).astype(jnp.bfloat16)
            w_own = jnp.exp2((s_own - top) * FACTOR).astype(jnp.bfloat16)
            mixed = jnp.dot(w_rest, VM[: CACHE + TOK], preferred_element_type=jnp.float32) + jnp.dot(
                w_own, VM[CACHE + TOK :], preferred_element_type=jnp.float32
            )
            O[h] = (mixed[:, :HEAD] / mixed[:, HEAD:]).astype(jnp.bfloat16)
        for h in heads:
            written(h).start()

    def written(h):
        return pltpu.make_async_copy(O.at[h], att.at[:, pl.ds(pl.multiple_of(h * HEAD, HEAD), HEAD)], out_sem.at[h])

    local["w1"].wait()
    a_z(1, 0)
    a_xsend(1, 0)
    local["w2"].wait()
    a_z(2, 0)
    W0[y, x, z] = KVW[kind]
    b_step(0)
    for name in ("counts", "place", "qg", "kg"):
        local[name].wait()
    a_z(1, 1)
    a_xsend(1, 1, 2)
    a_z(2, 1)
    a_xforward(1, 0)
    b_step(1)
    tables(y)
    a_z(1, 2)
    a_xsend(1, 3, 4)
    a_z(2, 2)
    a_xforward(1, 1, 2)
    b_step(2)
    tables(ym(1))
    a_z(1, 3)
    a_xsend(1, 5, 6)
    a_z(2, 3)
    a_xforward(1, 3, 4)
    b_step(3)
    tables(ym(-1))
    a_z(1, 4)
    a_xsend(1, 7)
    a_z(2, 4)
    b_step(4)
    a_xforward(1, 5, 6)
    a_xsend(2, 0, 1, 2, 3)
    tables(ym(2))
    for d in (0, 1):
        h_arrived(d, d)
    h_forward(0)
    h_forward(1)
    b_step(5)
    a_xforward(1, 7)
    a_xsend(2, 4, 5, 6, 7)
    row = lax.broadcasted_iota(jnp.int32, (TOK, TOK), 0)
    col = lax.broadcasted_iota(jnp.int32, (TOK, TOK), 1)
    TRI[...] = jnp.where(col <= row, 0.0, NEG)
    send(ck, KC.at[zp], kv_s.at[0], kv_r.at[0], pair)
    send(cv, VC.at[zp], kv_s.at[1], kv_r.at[1], pair)
    b_step(6)
    for d in (0, 1):
        h_arrived(d, 1 - d)
        h_to_core(d)
    a_end(1)
    for name in ("hid", "ck", "cv"):
        local[name].wait()
    h_from_core(y, 0)
    own_queries(1)
    NEW[kind, zp] = fresh(y)
    for d in (0, 1):
        h_from_core(side(d), 1 + d)
    PB[...] = fresh(ym(toward))
    send(PB, NEW.at[kind, zp], kv_s.at[4], kv_r.at[4], at(dy=toward))
    a_xforward(2, 0, 1)
    queries(ym(1), 1)
    q_send(0, 1)
    a_xforward(2, 2, 3)
    queries(ym(-1), 1)
    q_send(1, 1)
    a_xforward(2, 4, 5)
    arrived(NEW.at[1 - kind, zp], kv_s.at[4], kv_r.at[4])
    for n in (0, 1):
        send(NEW.at[n, zp], NEW.at[n, zp], kv_s.at[2 + n], kv_r.at[2 + n], pair)
    nk[...] = NEW[0, zp]
    nv[...] = NEW[1, zp]
    a_xforward(2, 6, 7)
    h_far(0)
    arrived(KC.at[1 - zp], kv_s.at[0], kv_r.at[0])
    arrived(VC.at[1 - zp], kv_s.at[1], kv_r.at[1])
    for n in (0, 1):
        arrived(NEW.at[n, 1 - zp], kv_s.at[2 + n], kv_r.at[2 + n])
    arrange_keys()
    q_wait(0, 1)
    attend(4 * y, 4 * y + 1, 4 * ym(-1), 4 * ym(-1) + 1)
    h_far(1)
    a_end(2)
    queries(ym(1), 2)
    q_send(0, 2)
    queries(ym(-1), 2)
    q_send(1, 2)
    h_far_from_core()
    queries(ym(2), 1)
    q_send(2, 1)
    queries(ym(2), 2)
    q_send(2, 2)
    own_queries(2)
    q_wait(1, 1)

    def four(n, carry):
        @pl.when(n == 1)
        def _():
            q_wait(0, 2)
            q_wait(1, 2)

        @pl.when(n == 2)
        def _():
            q_wait(2, 1)
            q_wait(2, 2)

        a = 4 * ((y + 1 + 2 * n - 3 * (n // 2)) % NY) + 2 * (n % 2)
        b = 4 * ((y + n) % NY) + 2
        attend(a, a + 1, b, b + 1)
        return carry

    lax.fori_loop(0, 3, four, 0)
    for h in range(4 * NY):
        written(h).wait()
    for copy in sent:
        copy.wait_send()


def on_device(hidden, w_query, key_weight, value_weight, q_gain, key_norm_gain, earlier_keys, earlier_values, counts, place):
    vmem = pl.BlockSpec(memory_space=pltpu.VMEM)
    hbm = pl.BlockSpec(memory_space=pltpu.HBM)
    bf16, f32 = jnp.bfloat16, jnp.float32
    dma = pltpu.SemaphoreType.DMA

    def both(*shape):
        return [dma(shape), dma(shape)]

    return pl.pallas_call(
        kernel,
        name="prefill",
        out_shape=(
            jax.ShapeDtypeStruct((TOK, 16 * HEAD), bf16),
            jax.ShapeDtypeStruct((TOK, HEAD), bf16),
            jax.ShapeDtypeStruct((TOK, HEAD), bf16),
        ),
        in_specs=[hbm] * 10,
        out_specs=(hbm, vmem, vmem),
        scratch_shapes=[
            pltpu.VMEM((NY, 2, TOK, 2048), bf16),
            pltpu.VMEM((2, NY, NX, NZ, 32, 256), bf16),
            pltpu.VMEM((NY, NX, NZ, 32, HEAD), bf16),
            pltpu.VMEM((2, 32, HEAD), bf16),
            pltpu.VMEM((2, 1024, HEAD), bf16),
            pltpu.VMEM((2, 1024, HEAD), bf16),
            pltpu.VMEM((2, 2, TOK, HEAD), bf16),
            pltpu.VMEM((TOK, HEAD), bf16),
            pltpu.VMEM((KEYS, HEAD), bf16),
            pltpu.VMEM((KEYS, 2 * HEAD), bf16),
            pltpu.VMEM((NY, 4, TOK, HEAD), bf16),
            pltpu.VMEM((16, TOK, HEAD), bf16),
            pltpu.VMEM((NY, TOK, HEAD), f32),
            pltpu.VMEM((NY, TOK, HEAD), f32),
            pltpu.VMEM((TOK, TOK), f32),
            pltpu.VMEM((16, TOK, HEAD), bf16),
            pltpu.SMEM((64,), jnp.int32),
            pltpu.VMEM((SLOTS, 64), jnp.int32),
            pltpu.VMEM((1, HEAD), f32),
            pltpu.VMEM((1, HEAD), f32),
            dma((11,)),
            dma((16,)),
            *both(3, 3),
            *both(3, 4),
            *both(7),
            *both(5),
            *both(2, 2, 4),
            *both(2, 3, 8),
            *both(4),
            *both(4, 2, 4),
            *both(3, 2),
        ],
        compiler_params=pltpu.CompilerParams(
            collective_id=0, has_side_effects=True, vmem_limit_bytes=52 << 20
        ),
    )(
        *(
            pltpu.with_memory_space_constraint(a, pltpu.HBM)
            for a in (
                counts,
                place.T,
                hidden,
                w_query,
                key_weight,
                value_weight,
                q_gain.reshape(1, HEAD),
                key_norm_gain.reshape(1, HEAD),
                earlier_keys,
                earlier_values,
            )
        )
    )


def solution(mesh):
    placed = (
        P("ctx", "tp"),
        P("ctx", "tp"),
        P("ctx", "tp"),
        P("ctx", "tp"),
        P(),
        P(),
        P("ctx", "tp"),
        P("ctx", "tp"),
        P(),
        P(),
    )
    return jax.shard_map(
        on_device,
        mesh=mesh,
        in_specs=placed,
        out_specs=(P("ctx", "tp"), P("ctx", "tp"), P("ctx", "tp")),
        check_vma=False,
    )
```

```python
import functools
import math

import jax
import jax.numpy as jnp
from jax import lax
from jax.experimental import pallas as pl
from jax.experimental.pallas import tpu as pltpu
from jax.sharding import PartitionSpec as P

MESH = pl.DeviceIdType.MESH
HEAD = 128
BLOCK = 128
TOK = 256
NY, NX, NZ = 4, 4, 8
SLOTS = 16
CACHE = SLOTS * BLOCK
KEYS = CACHE + 2 * TOK
FACTOR = HEAD**-0.5 * math.log2(math.e)
NEG = -1e30


def kernel(
    counts_in, place_in, hid, wq, kw, vw, qg_in, kg_in, ck, cv,
    att, new,
    H, W, W0, KVW, KC, VC, NEW, PB, KM, VM, QS, QA, COS, SIN, TRI, O, counts, place, qg, kg,
    local_sem, out_sem,
    p0_s, p0_r, h_s, h_r, c_s, c_r, kv_s, kv_r, za_s, za_r, xa_s, xa_r, xb_s, xb_r, zb_s, zb_r, q_s, q_r,
):
    i = lax.axis_index("ctx")
    c = lax.axis_index("tp")
    y, x, z = i // (NX * NZ), (i // NZ) % NX, i % NZ
    zp = z % 2
    kind = y % 2
    toward = 1 - 2 * kind
    sent = []

    def ym(k):
        return (y + k + NY) % NY

    def xm(k):
        return (x + k + NX) % NX

    def zm(k):
        return (z + k + NZ) % NZ

    def at(dy=0, dx=0, dz=0):
        return (ym(dy) * (NX * NZ) + xm(dx) * NZ + zm(dz), c)

    other_core = (i, 1 - c)
    pair = (i + 1 - 2 * zp, c)

    def send(src, dst, s, r, device):
        copy = pltpu.make_async_remote_copy(
            src_ref=src, dst_ref=dst, send_sem=s, recv_sem=r, device_id=device, device_id_type=MESH
        )
        copy.start()
        sent.append(copy)

    def arrived(dst, s, r):
        pltpu.make_async_remote_copy(
            src_ref=dst, dst_ref=dst, send_sem=s, recv_sem=r, device_id=other_core, device_id_type=MESH
        ).wait_recv()

    local = {}

    def bring(name, src, dst):
        copy = pltpu.make_async_copy(src, dst, local_sem.at[len(local)])
        copy.start()
        local[name] = copy

    def columns(yb, g):
        return pl.ds(pl.multiple_of(yb * 512 + (g - 1) * 256, 256), 256)

    bring("kw", kw, KVW.at[0])
    bring("vw", vw, KVW.at[1])
    bring("w1", wq.at[:, columns(y, 1)], W.at[0, y, x, z])
    bring("w2", wq.at[:, columns(y, 2)], W.at[1, y, x, z])
    bring("counts", counts_in, counts)
    bring("place", place_in, place)
    bring("qg", qg_in, qg)
    bring("kg", kg_in, kg)
    bring("hid", hid, H.at[y, c])
    bring("ck", ck, KC.at[zp])
    bring("cv", cv, VC.at[zp])

    barrier = pltpu.get_barrier_semaphore()
    for device in (at(dy=1), at(dy=-1), at(dy=2), at(dx=1), at(dx=-1), at(dz=1), at(dz=-1), other_core):
        pl.semaphore_signal(barrier, inc=1, device_id=device, device_id_type=MESH)
    pl.semaphore_wait(barrier, 8)

    steps_y = (1, -1, 2)

    def p0_queries(g):
        for n, dy in enumerate(steps_y):
            send(wq.at[:, columns(ym(dy), g)], W.at[g - 1, y, x, z], p0_s.at[n, g], p0_r.at[n, g], at(dy=dy))

    def p0_kv():
        for n, dy in enumerate(steps_y):
            send(KVW.at[ym(dy) % 2], W0.at[y, x, z], p0_s.at[n, 0], p0_r.at[n, 0], at(dy=dy))

    p0_queries(1)
    local["kw"].wait()
    local["vw"].wait()
    p0_kv()
    p0_queries(2)

    def own_rows(g):
        for n, dy in enumerate(steps_y):
            ref = W0.at[ym(-dy), x, z] if g == 0 else W.at[g - 1, ym(-dy), x, z]
            arrived(ref, p0_s.at[n, g], p0_r.at[n, g])

    def half(n):
        return pl.ds(128 * n, 128)

    def quarter(n):
        return pl.ds(64 * n, 64)

    for n in (0, 1):
        send(hid.at[half(n)], H.at[y, c, half(n)], h_s.at[0, n], h_r.at[0, n], at(dy=1))
        send(hid.at[half(1 - n)], H.at[y, c, half(1 - n)], h_s.at[1, 1 - n], h_r.at[1, 1 - n], at(dy=-1))
    send(hid, H.at[y, c], c_s.at[0], c_r.at[0], other_core)

    def side(d):
        return ym(-1 if d == 0 else 1)

    def h_arrived(d, n):
        arrived(H.at[side(d), c, half(n)], h_s.at[d, n], h_r.at[d, n])

    def h_forward(n):
        for d in (0, 1):
            ref = H.at[side(d), c, quarter(2 * d + n)]
            send(ref, ref, h_s.at[2, 2 * d + n], h_r.at[2, 2 * d + n], at(dy=1 if d == 0 else -1))

    def h_far(n):
        for d in (0, 1):
            ref = H.at[ym(2), c, quarter(2 * d + n)]
            arrived(ref, h_s.at[2, 2 * d + n], h_r.at[2, 2 * d + n])
            send(ref, ref, c_s.at[3 + 2 * d + n], c_r.at[3 + 2 * d + n], other_core)

    def h_far_from_core():
        for n in range(4):
            arrived(H.at[ym(2), 1 - c, quarter(n)], c_s.at[3 + n], c_r.at[3 + n])

    def h_to_core(d):
        send(H.at[side(d), c], H.at[side(d), c], c_s.at[1 + d], c_r.at[1 + d], other_core)

    def h_from_core(yb, slot):
        arrived(H.at[yb, 1 - c], c_s.at[slot], c_r.at[slot])

    def order(j):
        return zm((0, -1, 1, -2, 2, -3, 3, 4)[j])

    def a_block(g, xx, zz, hop=1, d=0):
        ref = W0 if g == 0 else W.at[g - 1]
        if hop == 4:
            return ref.at[pl.ds(2 * d, 2), xx, zz]
        return ref.at[:, xx, zz]

    def a_zsend(g, d, hop):
        sign = 1 - 2 * d
        ref = a_block(g, x, zm(-sign * (hop - 1)), hop, d)
        send(ref, ref, za_s.at[g - 1, d, hop - 1], za_r.at[g - 1, d, hop - 1], at(dz=sign))

    def a_zwait(g, d, hop):
        sign = 1 - 2 * d
        arrived(a_block(g, x, zm(-sign * hop), hop, d), za_s.at[g - 1, d, hop - 1], za_r.at[g - 1, d, hop - 1])

    def a_xsend(g, *blocks):
        for j in blocks:
            for d in (0, 1):
                ref = a_block(g, x, order(j))
                send(ref, ref, xa_s.at[g - 1, d, j], xa_r.at[g - 1, d, j], at(dx=1 - 2 * d))

    def a_xwait(g, d, j):
        arrived(a_block(g, xm(2 * d - 1), order(j)), xa_s.at[g - 1, d, j], xa_r.at[g - 1, d, j])

    def a_xforward(g, *blocks):
        for j in blocks:
            d = j % 2
            a_xwait(g, d, j)
            ref = a_block(g, xm(2 * d - 1), order(j))
            send(ref, ref, xa_s.at[g - 1, 2, j], xa_r.at[g - 1, 2, j], at(dx=1 - 2 * d))

    def a_z(g, n):
        if n == 0:
            own_rows(g)
        for d in (0, 1):
            if n:
                a_zwait(g, d, n)
            if n < 4:
                a_zsend(g, d, n + 1)

    def a_end(g):
        for j in range(8):
            a_xwait(g, 1 - j % 2, j)
            arrived(a_block(g, xm(2), order(j)), xa_s.at[g - 1, 2, j], xa_r.at[g - 1, 2, j])

    far = (0, -1, 1, 2)

    def b_zsend(n, hop):
        for d in (0, 1):
            sign = 1 - 2 * d
            ref = a_block(0, xm(far[n]), zm(-sign * (hop - 1)), hop, d)
            send(ref, ref, zb_s.at[n, d, hop - 1], zb_r.at[n, d, hop - 1], at(dz=sign))

    def b_zwait(n, hop):
        for d in (0, 1):
            sign = 1 - 2 * d
            arrived(a_block(0, xm(far[n]), zm(-sign * hop), hop, d), zb_s.at[n, d, hop - 1], zb_r.at[n, d, hop - 1])

    def b_step(n):
        if n == 0:
            own_rows(0)
            for d in (0, 1):
                ref = a_block(0, x, z)
                send(ref, ref, xb_s.at[d], xb_r.at[d], at(dx=1 - 2 * d))
            b_zsend(0, 1)
        elif n == 1:
            for d in (0, 1):
                arrived(a_block(0, xm(2 * d - 1), z), xb_s.at[d], xb_r.at[d])
                ref = a_block(0, xm(2 * d - 1), z, 4, d)
                send(ref, ref, xb_s.at[2 + d], xb_r.at[2 + d], at(dx=1 - 2 * d))
            b_zsend(1, 1)
            b_zsend(2, 1)
        elif n == 2:
            for d in (0, 1):
                arrived(a_block(0, xm(2), z, 4, d), xb_s.at[2 + d], xb_r.at[2 + d])
            b_zsend(3, 1)
        elif n <= 5:
            for m in range(4):
                b_zwait(m, n - 2)
                b_zsend(m, n - 1)
        else:
            for m in range(4):
                b_zwait(m, 4)

    def trajectory(yb):
        return (yb * (NX * NZ) + x * NZ + z) // 2

    def tables(yb):
        lane = lax.broadcasted_iota(jnp.int32, (TOK, HEAD), 1)
        freq = jnp.exp((lane % 64).astype(jnp.float32) * (-2.0 / HEAD) * math.log(1000000.0))
        start = counts[trajectory(yb)] * BLOCK + zp * TOK
        pos = (start + lax.broadcasted_iota(jnp.int32, (TOK, HEAD), 0)).astype(jnp.float32)
        angle = pos * freq
        COS[yb] = jnp.cos(angle)
        SIN[yb] = jnp.where(lane < 64, -1.0, 1.0) * jnp.sin(angle)

    def turned(v, gain, yb):
        v = v * lax.rsqrt(jnp.mean(v * v, axis=-1, keepdims=True) + 1e-06) * gain
        return (v * COS[yb] + pltpu.roll(v, 64, 1) * SIN[yb]).astype(jnp.bfloat16)

    def project(yb, w):
        rows, width = NY // 2 * NX * NZ * 32, w.shape[-1]
        low = jnp.dot(H[yb, 0], w[0:2].reshape(rows, width), preferred_element_type=jnp.float32)
        high = jnp.dot(H[yb, 1], w[2:4].reshape(rows, width), preferred_element_type=jnp.float32)
        return low + high

    def queries(yb, g):
        out = project(yb, W.at[g - 1])
        for h in (0, 1):
            QS[yb, 2 * (g - 1) + h] = turned(out[:, h * HEAD : (h + 1) * HEAD], qg[...], yb)

    def own_queries(g):
        queries(y, g)
        for h in (0, 1):
            QA[4 * y + 2 * (g - 1) + h] = QS[y, 2 * (g - 1) + h]

    def q_send(n, g):
        dy = steps_y[n]
        heads = pl.ds(2 * (g - 1), 2)
        send(QS.at[ym(dy), heads], QA.at[pl.ds(4 * y + 2 * (g - 1), 2)], q_s.at[n, g - 1], q_r.at[n, g - 1], at(dy=dy))

    def q_wait(n, g):
        arrived(QA.at[pl.ds(4 * ym(-steps_y[n]) + 2 * (g - 1), 2)], q_s.at[n, g - 1], q_r.at[n, g - 1])

    def fresh(yb):
        out = project(yb, W0)
        keys = jnp.full((TOK, HEAD), kind, jnp.int32) == 0
        return jnp.where(keys, turned(out, kg[...], yb).astype(jnp.float32), out).astype(jnp.bfloat16)

    def arrange_keys():
        b = trajectory(y)
        mine = lax.broadcasted_iota(jnp.int32, (SLOTS, 64), 1) == b
        slot_order = jnp.sum(jnp.where(mine, place[...].astype(jnp.float32), 0.0), axis=1, keepdims=True)
        used = lax.broadcasted_iota(jnp.int32, (SLOTS, 1), 0) < counts[b]
        first = jnp.broadcast_to(NEW[0, 0, 0:1, :].astype(jnp.float32), (BLOCK, HEAD))

        def put(at_row, on, k, v):
            KM[pl.ds(at_row, BLOCK), :] = jnp.where(on, k.astype(jnp.float32), first).astype(jnp.bfloat16)
            VM[pl.ds(at_row, BLOCK), 0:HEAD] = jnp.where(on, v.astype(jnp.float32), 0.0).astype(jnp.bfloat16)
            VM[pl.ds(at_row, BLOCK), HEAD : 2 * HEAD] = jnp.where(on, 1.0, 0.0).astype(jnp.bfloat16)

        for s in range(SLOTS):
            hit = jnp.where(used, jnp.where(slot_order == s, 1.0, 0.0), 0.0)
            on = jnp.broadcast_to(jnp.max(hit, axis=0, keepdims=True), (BLOCK, HEAD)) > 0.5
            rows = pl.ds(s % 8 * BLOCK, BLOCK)
            put(s * BLOCK, on, KC[s // 8, rows, :], VC[s // 8, rows, :])
        for s in range(2):
            rows = pl.ds(s * BLOCK, BLOCK)
            seen = jnp.full((BLOCK, HEAD), zp, jnp.int32) > 0
            put(CACHE + s * BLOCK, seen, NEW[0, 1 - zp, rows, :], NEW[1, 1 - zp, rows, :])
            put(CACHE + TOK + s * BLOCK, seen | True, NEW[0, zp, rows, :], NEW[1, zp, rows, :])

    def attend(*heads):
        scores = []
        for h in heads:
            s = lax.dot_general(QA[h], KM[...], (((1,), (1,)), ((), ())), preferred_element_type=jnp.float32)
            s_own = s[:, CACHE + TOK :] + TRI[...]
            s_rest = s[:, : CACHE + TOK]
            top = jnp.maximum(jnp.max(s_rest, axis=-1, keepdims=True), jnp.max(s_own, axis=-1, keepdims=True))
            scores.append((s_rest, s_own, top))
        for h, (s_rest, s_own, top) in zip(heads, scores):
            w_rest = jnp.exp2((s_rest - top) * FACTOR).astype(jnp.bfloat16)
            w_own = jnp.exp2((s_own - top) * FACTOR).astype(jnp.bfloat16)
            mixed = jnp.dot(w_rest, VM[: CACHE + TOK], preferred_element_type=jnp.float32) + jnp.dot(
                w_own, VM[CACHE + TOK :], preferred_element_type=jnp.float32
            )
            O[h] = (mixed[:, :HEAD] / mixed[:, HEAD:]).astype(jnp.bfloat16)
        for h in heads:
            written(h).start()

    def written(h):
        return pltpu.make_async_copy(O.at[h], att.at[:, pl.ds(pl.multiple_of(h * HEAD, HEAD), HEAD)], out_sem.at[h])

    local["w1"].wait()
    a_z(1, 0)
    a_xsend(1, 0)
    local["w2"].wait()
    a_z(2, 0)
    W0[y, x, z] = KVW[kind]
    b_step(0)
    for name in ("counts", "place", "qg", "kg"):
        local[name].wait()
    a_z(1, 1)
    a_xsend(1, 1, 2)
    a_z(2, 1)
    a_xforward(1, 0)
    b_step(1)
    tables(y)
    a_z(1, 2)
    a_xsend(1, 3, 4)
    a_z(2, 2)
    a_xforward(1, 1, 2)
    b_step(2)
    tables(ym(1))
    a_z(1, 3)
    a_xsend(1, 5, 6)
    a_z(2, 3)
    a_xforward(1, 3, 4)
    b_step(3)
    tables(ym(-1))
    a_z(1, 4)
    a_xsend(1, 7)
    a_z(2, 4)
    b_step(4)
    a_xforward(1, 5, 6)
    a_xsend(2, 0, 1, 2, 3)
    tables(ym(2))
    for d in (0, 1):
        h_arrived(d, d)
    h_forward(0)
    h_forward(1)
    b_step(5)
    a_xforward(1, 7)
    a_xsend(2, 4, 5, 6, 7)
    row = lax.broadcasted_iota(jnp.int32, (TOK, TOK), 0)
    col = lax.broadcasted_iota(jnp.int32, (TOK, TOK), 1)
    TRI[...] = jnp.where(col <= row, 0.0, NEG)
    send(ck, KC.at[zp], kv_s.at[0], kv_r.at[0], pair)
    send(cv, VC.at[zp], kv_s.at[1], kv_r.at[1], pair)
    b_step(6)
    for d in (0, 1):
        h_arrived(d, 1 - d)
        h_to_core(d)
    a_end(1)
    for name in ("hid", "ck", "cv"):
        local[name].wait()
    h_from_core(y, 0)
    own_queries(1)
    NEW[kind, zp] = fresh(y)
    for d in (0, 1):
        h_from_core(side(d), 1 + d)
    PB[...] = fresh(ym(toward))
    send(PB, NEW.at[kind, zp], kv_s.at[4], kv_r.at[4], at(dy=toward))
    a_xforward(2, 0, 1)
    queries(ym(1), 1)
    q_send(0, 1)
    a_xforward(2, 2, 3)
    queries(ym(-1), 1)
    q_send(1, 1)
    a_xforward(2, 4, 5)
    arrived(NEW.at[1 - kind, zp], kv_s.at[4], kv_r.at[4])
    for n in (0, 1):
        send(NEW.at[n, zp], NEW.at[n, zp], kv_s.at[2 + n], kv_r.at[2 + n], pair)
    new[0] = NEW[0, zp]
    new[1] = NEW[1, zp]
    a_xforward(2, 6, 7)
    h_far(0)
    arrived(KC.at[1 - zp], kv_s.at[0], kv_r.at[0])
    arrived(VC.at[1 - zp], kv_s.at[1], kv_r.at[1])
    for n in (0, 1):
        arrived(NEW.at[n, 1 - zp], kv_s.at[2 + n], kv_r.at[2 + n])
    arrange_keys()
    q_wait(0, 1)
    attend(4 * y, 4 * y + 1, 4 * ym(-1), 4 * ym(-1) + 1)
    h_far(1)
    a_end(2)
    queries(ym(1), 2)
    q_send(0, 2)
    queries(ym(-1), 2)
    q_send(1, 2)
    h_far_from_core()
    queries(ym(2), 1)
    q_send(2, 1)
    queries(ym(2), 2)
    q_send(2, 2)
    own_queries(2)
    q_wait(1, 1)

    def four(n, carry):
        @pl.when(n == 1)
        def _():
            q_wait(0, 2)
            q_wait(1, 2)

        @pl.when(n == 2)
        def _():
            q_wait(2, 1)
            q_wait(2, 2)

        a = 4 * ((y + 1 + 2 * n - 3 * (n // 2)) % NY) + 2 * (n % 2)
        b = 4 * ((y + n) % NY) + 2
        attend(a, a + 1, b, b + 1)
        return carry

    lax.fori_loop(0, 3, four, 0)
    for h in range(4 * NY):
        written(h).wait()
    for copy in sent:
        copy.wait_send()


def on_device(hidden, w_query, key_weight, value_weight, q_gain, key_norm_gain, earlier_keys, earlier_values, counts, place):
    vmem = pl.BlockSpec(memory_space=pltpu.VMEM)
    hbm = pl.BlockSpec(memory_space=pltpu.HBM)
    bf16, f32 = jnp.bfloat16, jnp.float32
    dma = pltpu.SemaphoreType.DMA

    def both(*shape):
        return [dma(shape), dma(shape)]

    attended, new = pl.pallas_call(
        kernel,
        name="prefill",
        out_shape=(
            jax.ShapeDtypeStruct((TOK, 16 * HEAD), bf16),
            jax.ShapeDtypeStruct((2, TOK, HEAD), bf16),
        ),
        in_specs=[hbm] * 10,
        out_specs=(hbm, vmem),
        scratch_shapes=[
            pltpu.VMEM((NY, 2, TOK, 2048), bf16),
            pltpu.VMEM((2, NY, NX, NZ, 32, 256), bf16),
            pltpu.VMEM((NY, NX, NZ, 32, HEAD), bf16),
            pltpu.VMEM((2, 32, HEAD), bf16),
            pltpu.VMEM((2, 1024, HEAD), bf16),
            pltpu.VMEM((2, 1024, HEAD), bf16),
            pltpu.VMEM((2, 2, TOK, HEAD), bf16),
            pltpu.VMEM((TOK, HEAD), bf16),
            pltpu.VMEM((KEYS, HEAD), bf16),
            pltpu.VMEM((KEYS, 2 * HEAD), bf16),
            pltpu.VMEM((NY, 4, TOK, HEAD), bf16),
            pltpu.VMEM((16, TOK, HEAD), bf16),
            pltpu.VMEM((NY, TOK, HEAD), f32),
            pltpu.VMEM((NY, TOK, HEAD), f32),
            pltpu.VMEM((TOK, TOK), f32),
            pltpu.VMEM((16, TOK, HEAD), bf16),
            pltpu.SMEM((64,), jnp.int32),
            pltpu.VMEM((SLOTS, 64), jnp.int32),
            pltpu.VMEM((1, HEAD), f32),
            pltpu.VMEM((1, HEAD), f32),
            dma((11,)),
            dma((16,)),
            *both(3, 3),
            *both(3, 4),
            *both(7),
            *both(5),
            *both(2, 2, 4),
            *both(2, 3, 8),
            *both(4),
            *both(4, 2, 4),
            *both(3, 2),
        ],
        compiler_params=pltpu.CompilerParams(
            collective_id=0, has_side_effects=True, vmem_limit_bytes=52 << 20
        ),
    )(
        *(
            pltpu.with_memory_space_constraint(a, pltpu.HBM)
            for a in (
                counts,
                place.T,
                hidden,
                w_query,
                key_weight,
                value_weight,
                q_gain.reshape(1, HEAD),
                key_norm_gain.reshape(1, HEAD),
                earlier_keys,
                earlier_values,
            )
        )
    )
    return attended, new[0], new[1]


def solution(mesh):
    placed = (
        P("ctx", "tp"),
        P("ctx", "tp"),
        P("ctx", "tp"),
        P("ctx", "tp"),
        P(),
        P(),
        P("ctx", "tp"),
        P("ctx", "tp"),
        P(),
        P(),
    )
    return jax.shard_map(
        on_device,
        mesh=mesh,
        in_specs=placed,
        out_specs=(P("ctx", "tp"), P("ctx", "tp"), P("ctx", "tp")),
        check_vma=False,
    )
```
